32 devices in a mesh: grp: 2 (over y), ev: 2 (over x), loc: 8 (over z, core).
Axes of the slice: x: 2, y: 2, z: 4, core: 2. Of those that a mesh axis runs over, the one named last changes fastest.
Arguments:
- intensity_bin: int32 [256, 16384], P('ev', ('grp', 'loc')), parts along dimension 1, may hold values from 0 to 62
- bin_fraction: bfloat16 [256, 16384], P('ev', ('grp', 'loc')), parts along dimension 1, may hold values from 0 to 1
- footprint_mask: int32 [256, 128], P('ev', ('grp', 'loc')), parts along dimension 1, may hold values 0 or 1
- location_contract: int32 [16384], P(('grp', 'loc')), parts along dimension 0, may hold values from 0 to 2047
- location_class: int32 [16384], P(('grp', 'loc')), parts along dimension 0, may hold values from 0 to 127
- exposure: float32 [16384], P(('grp', 'loc')), parts along dimension 0, may hold values from 0.32 to 3.2
- curves: float32 [128, 64], replicated, may hold values from 0 to 1
- event_year: int32 [256], P('ev'), may hold values from 0 to 127
- occ_retention: float32 [4096], P('grp'), parts along dimension 0, may hold values from 0.2 to 0.8
- occ_limit: float32 [4096], P('grp'), parts along dimension 0, may hold values from 0.8 to 2.5
- agg_retention: float32 [4096], P('grp'), parts along dimension 0, may hold values from 0.125 to 0.375
- agg_limit: float32 [4096], P('grp'), parts along dimension 0, may hold values from 0.375 to 1
Outputs:
- annual: float32 [4096, 128], P(('grp', 'loc'), 'ev'), parts along dimension 0
- year_mean: float32 [256], P(('grp', 'ev')), parts along dimension 0
The draws below stay inside these ranges and needn't reach their ends.
There are 2 independent parts, one for each index of `grp`. The reference program is written for one: setup_inputs(seed, part) draws one part's arguments, and reference() takes and returns one part's arrays. A program takes and returns all parts, laid end to end along the dimension named above; an argument that names none is the same for every part. Nothing has to cross between parts.
All inputs are finite; a program needn't handle non-finite values. No bound on the sum of `footprint_mask` on one device may be relied on, other than what follows from the above.
Results may differ from the reference program's by a relative error of at most 0.0016.
Values sent between devices are 32-bit elements; how exact they have to be, the bound alone decides.
No kernel may reach another device: no remote copies, remote signals or barrier semaphores. Data moves between devices by JAX's collectives and lax.ppermute only.
A program may use at most 64 MiB of HBM per device.

```python
import math
import jax
import jax.numpy as jnp
from jax import lax

CONTRACTS = 2048
KNOTS = 64
CURVES = 128
BLOCK = 128
EVENTS = 256
LOCATIONS = 8192
YEARS = 128


def plant(result, own_key, least, top_value):
    place = [jax.random.randint(jax.random.fold_in(own_key, axis), (), 0, length) for axis, length in enumerate(result.shape)]
    widest = result.shape.index(max(result.shape))
    next_to = place[:widest] + [(place[widest] + 1) % result.shape[widest]] + place[widest + 1:]
    return result.at[tuple(place)].set(least).at[tuple(next_to)].set(top_value)


def block_levels(key, shape, cuts, least, largest):
    def one(position, parts):
        steps = jax.random.uniform(jax.random.fold_in(jax.random.fold_in(key, 6), position), (parts,), jnp.float32, least / len(cuts), largest / len(cuts))
        return jnp.repeat(jnp.exp(steps), shape[position] // parts).reshape((-1,) + (1,) * (len(shape) - position - 1))

    factor_of = one(*cuts[0])
    for cut in cuts[1:]:
        factor_of = factor_of * one(*cut)
    return factor_of


def setup_inputs(seed: int = 0, part: int = 0) -> dict:
    key_list = jax.random.split(jax.random.key(seed), 13)
    own_keys = jax.random.split(jax.random.fold_in(key_list[12], part), 13)
    return {
        "intensity_bin": plant(jax.random.randint(own_keys[0], (EVENTS, LOCATIONS), 0, KNOTS - 1), jax.random.fold_in(own_keys[0], 1), 0, (KNOTS - 1) - 1).astype(jnp.int32),
        "bin_fraction": jnp.clip(1.0 * jax.random.uniform(own_keys[1], (EVENTS, LOCATIONS), jnp.float32) ** block_levels(own_keys[1], (EVENTS, LOCATIONS), ((0, 2), (1, 8)), -0.2, 0.2), 0.0, 1.0).astype(jnp.bfloat16),
        "footprint_mask": plant((jax.random.randint(own_keys[2], (EVENTS, LOCATIONS // BLOCK), 0, 2) < 1).astype(jnp.int32), jax.random.fold_in(own_keys[2], 1), 0, 1),
        "location_contract": plant(jax.random.randint(own_keys[3], (LOCATIONS,), 0, CONTRACTS), jax.random.fold_in(own_keys[3], 1), 0, CONTRACTS - 1).astype(jnp.int32),
        "location_class": plant(jax.random.randint(own_keys[4], (LOCATIONS,), 0, CURVES), jax.random.fold_in(own_keys[4], 1), 0, CURVES - 1).astype(jnp.int32),
        "exposure": jnp.clip(jnp.exp(math.log(3.2) - 2.3025851 * jax.random.uniform(own_keys[5], (LOCATIONS,), jnp.float32) ** block_levels(own_keys[5], (LOCATIONS,), ((0, 8),), -0.2, 0.2)), 0.32, 3.2),
        "curves": jnp.clip(jax.random.uniform(key_list[6], (CURVES, KNOTS), jnp.float32, 0.0, 1.0), 0.0, 1.0),
        "event_year": plant(jax.random.randint(key_list[7], (EVENTS,), 0, YEARS), jax.random.fold_in(key_list[7], 1), 0, YEARS - 1).astype(jnp.int32),
        "occ_retention": jnp.clip(jax.random.uniform(own_keys[8], (CONTRACTS,), jnp.float32, 0.2, 0.8), 0.2, 0.8),
        "occ_limit": jnp.clip(jax.random.uniform(own_keys[9], (CONTRACTS,), jnp.float32, 0.8, 2.5), 0.8, 2.5),
        "agg_retention": jnp.clip(jax.random.uniform(own_keys[10], (CONTRACTS,), jnp.float32, 0.125, 0.375), 0.125, 0.375),
        "agg_limit": jnp.clip(jax.random.uniform(own_keys[11], (CONTRACTS,), jnp.float32, 0.375, 1.0), 0.375, 1.0),
    }


def reference(intensity_bin, bin_fraction, footprint_mask, location_contract, location_class, exposure, curves, event_year, occ_retention, occ_limit, agg_retention, agg_limit):
    curve_rows = curves[location_class]
    width = math.gcd(EVENTS, 64)
    count = EVENTS // width
    bins_all = intensity_bin.reshape(count, width, LOCATIONS)
    frac_all = bin_fraction.reshape(count, width, LOCATIONS)
    mask_all = footprint_mask.reshape(count, width, LOCATIONS // BLOCK)
    places = jnp.arange(LOCATIONS, dtype=jnp.int32)[None, :]

    def one_block(pieces):
        bins, frac, mask = pieces
        low = curve_rows[places, bins]
        high = curve_rows[places, bins + 1]
        fval = frac.astype(jnp.float32)
        damage = (1.0 - fval) * low + fval * high
        keep = jnp.repeat(mask.astype(jnp.float32), BLOCK, axis=1)
        loss = (damage * keep * exposure[None, :]).astype(jnp.bfloat16)
        return jax.ops.segment_sum(loss.astype(jnp.float32).T, location_contract, num_segments=CONTRACTS)

    blocks = lax.map(one_block, (bins_all, frac_all, mask_all))
    totals = jnp.transpose(blocks, (1, 0, 2)).reshape(CONTRACTS, EVENTS)
    occurrence = jnp.minimum(jnp.maximum(totals - occ_retention[:, None], 0.0), occ_limit[:, None])
    year_onehot = (event_year[:, None] == jnp.arange(YEARS, dtype=jnp.int32)[None, :]).astype(jnp.float32)
    yearly = jnp.dot(occurrence, year_onehot, precision=lax.Precision.HIGHEST, preferred_element_type=jnp.float32)
    annual = jnp.minimum(jnp.maximum(yearly - agg_retention[:, None], 0.0), agg_limit[:, None])
    year_mean = jnp.sum(annual, axis=0) / CONTRACTS
    return annual, year_mean
```

```python
import functools

import jax
import jax.numpy as jnp
from jax import lax
from jax.experimental import pallas as pl
from jax.experimental.pallas import tpu as pltpu
from jax.sharding import PartitionSpec as P

YR_DEV = 64
LANES = 128
SUBLANES = 8
CORES = 2

f32, bf16, i32 = jnp.float32, jnp.bfloat16, jnp.int32
HBM = pl.BlockSpec(memory_space=pltpu.HBM)
VMEM = pl.BlockSpec(memory_space=pltpu.VMEM)


def split3(x):
    a = x.astype(bf16)
    rest = x - a.astype(f32)
    b = rest.astype(bf16)
    rest = rest - b.astype(f32)
    return a, b, rest.astype(bf16)


def take_rows(x, index):
    return jnp.take_along_axis(x, index, axis=0, mode="promise_in_bounds")


def start_all(pairs, sems):
    copies = [pltpu.make_async_copy(src, dst, sems.at[i]) for i, (src, dst) in enumerate(pairs)]
    for copy in copies:
        copy.start()
    return copies


def member_rows(contract_ref, first, share):
    rows = lax.broadcasted_iota(i32, (share, LANES), 0)
    return jnp.concatenate(
        [
            (rows == contract_ref[j : j + 1, :] - first).astype(bf16)
            for j in range(contract_ref.shape[0])
        ],
        axis=1,
    )


def block_totals(contract_ref, loss, first, share):
    return lax.dot_general(
        loss,
        member_rows(contract_ref, first, share),
        (((1,), (1,)), ((), ())),
        preferred_element_type=f32,
    )


def damage_kernel(
    share, parts, bins_h, frac_h, mask_h, class_h, exposure_h, curve_h, contract_h,
    year_h, send_ref, loss_ref, contract_s, year_s,
    bins, frac, mask_s, class_s, exposure_s, curve_s, table, sems,
):
    events, locations = bins.shape
    knots, curves = curve_s.shape
    tiles = locations // LANES
    width = locations // parts
    small = start_all(
        [(class_h, class_s), (curve_h, curve_s), (mask_h, mask_s), (exposure_h, exposure_s),
         (contract_h, contract_s), (year_h, year_s)],
        sems,
    )
    large = start_all(
        [
            (src.at[:, p * width : (p + 1) * width], dst.at[:, p * width : (p + 1) * width])
            for p in range(parts)
            for src, dst in ((bins_h, bins), (frac_h, frac))
        ],
        sems.at[pl.ds(len(small), 2 * parts)],
    )
    for copy in small:
        copy.wait()
    low = curve_s[...]
    high = jnp.concatenate([low[1:], low[:1]], axis=0)
    terms = jnp.concatenate(split3(jnp.concatenate([low, high], axis=0)), axis=1)
    for j in range(tiles):
        onehot = (
            lax.broadcasted_iota(i32, (curves, LANES), 0) == class_s[j : j + 1, :]
        ).astype(bf16)
        table[:, j * LANES : (j + 1) * LANES] = jnp.dot(
            terms, jnp.concatenate([onehot] * 3, axis=0), preferred_element_type=f32
        )
    mask = mask_s[...].astype(f32).T
    groups = knots // SUBLANES
    for j in range(tiles):
        if j % (tiles // parts) == 0:
            for copy in large[2 * (j // (tiles // parts)) :][:2]:
                copy.wait()
        cols = slice(j * LANES, (j + 1) * LANES)
        lows = [table[SUBLANES * v : SUBLANES * (v + 1), cols] for v in range(groups)]
        highs = [
            table[knots + SUBLANES * v : knots + SUBLANES * (v + 1), cols] for v in range(groups)
        ]
        exposure = jnp.broadcast_to(exposure_s[j : j + 1, :], (SUBLANES, LANES))
        out = []
        for i in range(events // SUBLANES):
            rows = slice(SUBLANES * i, SUBLANES * (i + 1))
            knot = bins[rows, cols]
            within = knot & (SUBLANES - 1)
            group = knot // SUBLANES
            bits = [(group & (1 << q)) != 0 for q in range((groups - 1).bit_length())]

            def pick(tables):
                values = [take_rows(x, within) for x in tables]
                for bit in bits:
                    pairs = [values[q : q + 2] for q in range(0, len(values), 2)]
                    values = [jnp.where(bit, p[1], p[0]) if len(p) == 2 else p[0] for p in pairs]
                return values[0]

            weight = frac[rows, cols].astype(f32)
            damage = (1.0 - weight) * pick(lows) + weight * pick(highs)
            keep = jnp.broadcast_to(mask[rows, j : j + 1], (SUBLANES, LANES))
            out.append(damage * keep * exposure)
        loss_ref[:, cols] = jnp.concatenate(out, axis=0).astype(bf16)
    loc_count = lax.axis_size("loc")
    chips = loc_count // CORES
    me = lax.axis_index("loc")
    chip, core = me // CORES, lax.rem(me, CORES)
    loss = loss_ref[...]
    for k in range(chips):
        owner = lax.rem(chip + k, chips) * CORES + (1 - core)
        send_ref[k] = block_totals(contract_s, loss, owner * share, share)


def own_kernel(share, contract_s, loss_ref, out_ref):
    chips = out_ref.shape[0]
    me = lax.axis_index("loc")
    chip, core = me // CORES, lax.rem(me, CORES)
    loss = loss_ref[...]
    for k in range(chips):
        owner = lax.rem(chip + k, chips) * CORES + core
        out_ref[k] = block_totals(contract_s, loss, owner * share, share)


def year_kernel(count, *refs):
    ins, (terms_ref, year_ref), outs = (
        refs[:count], refs[count : count + 2], refs[count + 2 :]
    )
    total = ins[0][...]
    for ref in ins[1:]:
        total = total + ref[...]
    occurrence = jnp.minimum(jnp.maximum(total - terms_ref[0:1, :], 0.0), terms_ref[1:2, :])
    evs = len(outs)
    events = total.shape[0]
    ev = lax.axis_index("ev")
    for m, out in enumerate(outs):
        first = lax.rem(ev + m, evs) * YR_DEV
        years = lax.broadcasted_iota(i32, (YR_DEV, events), 0) + first
        onehot = (years == year_ref[...]).astype(f32)
        out[...] = jnp.dot(
            onehot, occurrence, precision=lax.Precision.HIGHEST, preferred_element_type=f32
        )


def annual_kernel(count, *refs):
    ins, (terms_ref, annual_ref, part_ref) = refs[:count], refs[count:]
    yearly = ins[0][...]
    for ref in ins[1:]:
        yearly = yearly + ref[...]
    annual = jnp.minimum(jnp.maximum(yearly - terms_ref[2:3, :], 0.0), terms_ref[3:4, :])
    annual_ref[...] = annual
    ones = jnp.ones((SUBLANES, annual.shape[1]), f32)
    part = lax.dot_general(
        ones, annual, (((1,), (1,)), ((), ())),
        precision=lax.Precision.HIGHEST, preferred_element_type=f32,
    )
    part_ref[...] = part[0:1, :]


def params(mib):
    return pltpu.CompilerParams(vmem_limit_bytes=mib << 20)


def rotate(size, k):
    return [(i, (i + k) % size) for i in range(size)]


def local(
    intensity_bin, bin_fraction, footprint_mask, location_contract, location_class, exposure,
    curves, event_year, occ_retention, occ_limit, agg_retention, agg_limit,
):
    events, locations = intensity_bin.shape
    curve_count, knots = curves.shape
    contract_count = occ_retention.shape[0]
    loc_count = lax.axis_size("loc")
    evs = lax.axis_size("ev")
    chips = loc_count // CORES
    share = contract_count // loc_count
    tiles = locations // LANES
    parts = 4
    dma = pltpu.SemaphoreType.DMA
    send, loss, contract_v, year_v = pl.pallas_call(
        functools.partial(damage_kernel, share, parts),
        out_shape=(
            jax.ShapeDtypeStruct((chips, events, share), f32),
            jax.ShapeDtypeStruct((events, locations), bf16),
            jax.ShapeDtypeStruct((tiles, LANES), i32),
            jax.ShapeDtypeStruct((1, events), i32),
        ),
        in_specs=[HBM] * 8,
        out_specs=(VMEM,) * 4,
        scratch_shapes=[
            pltpu.VMEM((events, locations), i32),
            pltpu.VMEM((events, locations), bf16),
            pltpu.VMEM((tiles, events), i32),
            pltpu.VMEM((tiles, LANES), i32),
            pltpu.VMEM((tiles, LANES), f32),
            pltpu.VMEM((knots, curve_count), f32),
            pltpu.VMEM((2 * knots, locations), f32),
            dma((6 + 2 * parts,)),
        ],
        compiler_params=params(24),
        cost_estimate=pl.CostEstimate(flops=10**9, bytes_accessed=2 << 20, transcendentals=0),
        name="damage",
    )(
        *(
            pltpu.with_memory_space_constraint(x, pltpu.HBM)
            for x in (
                intensity_bin, bin_fraction, footprint_mask.T,
                location_class.reshape(tiles, LANES), exposure.reshape(tiles, LANES), curves.T,
                location_contract.reshape(tiles, LANES), event_year.reshape(1, events),
            )
        )
    )
    partner = [(i, i ^ 1) for i in range(loc_count)]
    got = lax.ppermute(send, "loc", partner)
    own = pl.pallas_call(
        functools.partial(own_kernel, share),
        out_shape=jax.ShapeDtypeStruct((chips, events, share), f32),
        in_specs=[VMEM, VMEM],
        out_specs=VMEM,
        compiler_params=params(16),
        cost_estimate=pl.CostEstimate(flops=10**9, bytes_accessed=2 << 20, transcendentals=0),
        name="own_part",
    )(contract_v, loss)
    blocks = [own[0], got[0]]
    for k in range(chips - 1, 0, -1):
        pairs = [
            (i, ((i // CORES + k) % chips) * CORES + i % CORES) for i in range(loc_count)
        ]
        blocks.append(lax.ppermute(own[k] + got[k], "loc", pairs))
    first = lax.axis_index("loc") * share
    terms = lax.dynamic_slice(
        jnp.stack([occ_retention, occ_limit, agg_retention, agg_limit]), (0, first), (4, share)
    )
    yearly = pl.pallas_call(
        functools.partial(year_kernel, len(blocks)),
        out_shape=tuple(jax.ShapeDtypeStruct((YR_DEV, share), f32) for _ in range(evs)),
        in_specs=[VMEM] * (len(blocks) + 2),
        out_specs=tuple(VMEM for _ in range(evs)),
        compiler_params=params(16),
        name="years",
    )(*blocks, terms, year_v)
    sums = [yearly[0]] + [
        lax.ppermute(yearly[m], "ev", rotate(evs, m)) for m in range(1, evs)
    ]
    annual, part = pl.pallas_call(
        functools.partial(annual_kernel, len(sums)),
        out_shape=(
            jax.ShapeDtypeStruct((YR_DEV, share), f32),
            jax.ShapeDtypeStruct((1, YR_DEV), f32),
        ),
        in_specs=[VMEM] * (len(sums) + 1),
        out_specs=(VMEM, VMEM),
        compiler_params=params(16),
        name="annual",
    )(*sums, terms)
    mean = part.reshape(YR_DEV)
    if loc_count & (loc_count - 1) == 0:
        step = 1
        while step < loc_count:
            mean = mean + lax.ppermute(mean, "loc", [(i, i ^ step) for i in range(loc_count)])
            step *= 2
    else:
        mean = lax.psum(mean, "loc")
    return annual.T, mean / contract_count


def solution(mesh):
    in_specs = (
        P("ev", ("grp", "loc")),
        P("ev", ("grp", "loc")),
        P("ev", ("grp", "loc")),
        P(("grp", "loc")),
        P(("grp", "loc")),
        P(("grp", "loc")),
        P(),
        P("ev"),
        P("grp"),
        P("grp"),
        P("grp"),
        P("grp"),
    )
    out_specs = (P(("grp", "loc"), "ev"), P(("grp", "ev")))
    return jax.shard_map(local, mesh=mesh, in_specs=in_specs, out_specs=out_specs, check_vma=False)
```

```python
import functools

import jax
import jax.numpy as jnp
from jax import lax
from jax.experimental import pallas as pl
from jax.experimental.pallas import tpu as pltpu
from jax.sharding import PartitionSpec as P

YR_DEV = 64
LANES = 128
SUBLANES = 8
CORES = 2
HYBRID = False

f32, bf16, i32 = jnp.float32, jnp.bfloat16, jnp.int32
HBM = pl.BlockSpec(memory_space=pltpu.HBM)
VMEM = pl.BlockSpec(memory_space=pltpu.VMEM)


def split3(x):
    a = x.astype(bf16)
    rest = x - a.astype(f32)
    b = rest.astype(bf16)
    rest = rest - b.astype(f32)
    return a, b, rest.astype(bf16)


def take_rows(x, index):
    return jnp.take_along_axis(x, index, axis=0, mode="promise_in_bounds")


def start_all(pairs, sems):
    copies = [pltpu.make_async_copy(src, dst, sems.at[i]) for i, (src, dst) in enumerate(pairs)]
    for copy in copies:
        copy.start()
    return copies


def member_rows(contract_ref, first, share):
    rows = lax.broadcasted_iota(i32, (share, LANES), 0)
    return jnp.concatenate(
        [
            (rows == contract_ref[j : j + 1, :] - first).astype(bf16)
            for j in range(contract_ref.shape[0])
        ],
        axis=1,
    )


def block_totals(contract_ref, loss, first, share):
    return lax.dot_general(
        loss,
        member_rows(contract_ref, first, share),
        (((1,), (1,)), ((), ())),
        preferred_element_type=f32,
    )


def chip_at(chip, k, chips):
    if chips & (chips - 1) == 0:
        return chip ^ k
    return lax.rem(chip + k, chips)


def damage_kernel(
    share, parts, bins_h, frac_h, mask_h, class_h, exposure_h, curve_h, contract_h,
    year_h, send_ref, loss_ref, contract_s, year_s,
    bins, frac, mask_s, class_s, exposure_s, curve_s, table, sems,
):
    events, locations = bins.shape
    knots, curves = curve_s.shape
    tiles = locations // LANES
    width = locations // parts
    small = start_all(
        [(class_h, class_s), (curve_h, curve_s), (mask_h, mask_s), (exposure_h, exposure_s),
         (contract_h, contract_s), (year_h, year_s)],
        sems,
    )
    large = start_all(
        [
            (src.at[:, p * width : (p + 1) * width], dst.at[:, p * width : (p + 1) * width])
            for p in range(parts)
            for src, dst in ((bins_h, bins), (frac_h, frac))
        ],
        sems.at[pl.ds(len(small), 2 * parts)],
    )
    for copy in small:
        copy.wait()
    low = curve_s[...]
    high = jnp.concatenate([low[1:], low[:1]], axis=0)
    terms = jnp.concatenate(split3(jnp.concatenate([low, high], axis=0)), axis=1)
    for j in range(tiles):
        onehot = (
            lax.broadcasted_iota(i32, (curves, LANES), 0) == class_s[j : j + 1, :]
        ).astype(bf16)
        table[:, j * LANES : (j + 1) * LANES] = jnp.dot(
            terms, jnp.concatenate([onehot] * 3, axis=0), preferred_element_type=f32
        )
    mask = mask_s[...].astype(f32).T
    groups = knots // SUBLANES
    for j in range(tiles):
        if j % (tiles // parts) == 0:
            for copy in large[2 * (j // (tiles // parts)) :][:2]:
                copy.wait()
        cols = slice(j * LANES, (j + 1) * LANES)
        lows = [table[SUBLANES * v : SUBLANES * (v + 1), cols] for v in range(groups)]
        highs = [
            table[knots + SUBLANES * v : knots + SUBLANES * (v + 1), cols] for v in range(groups)
        ]
        exposure = jnp.broadcast_to(exposure_s[j : j + 1, :], (SUBLANES, LANES))
        out = []
        for i in range(events // SUBLANES):
            rows = slice(SUBLANES * i, SUBLANES * (i + 1))
            knot = bins[rows, cols]
            within = knot & (SUBLANES - 1)
            group = knot // SUBLANES
            bits = [(group & (1 << q)) != 0 for q in range((groups - 1).bit_length())]

            def pick(tables):
                values = [take_rows(x, within) for x in tables]
                for bit in bits:
                    pairs = [values[q : q + 2] for q in range(0, len(values), 2)]
                    values = [jnp.where(bit, p[1], p[0]) if len(p) == 2 else p[0] for p in pairs]
                return values[0]

            weight = frac[rows, cols].astype(f32)
            damage = (1.0 - weight) * pick(lows) + weight * pick(highs)
            keep = jnp.broadcast_to(mask[rows, j : j + 1], (SUBLANES, LANES))
            out.append(damage * keep * exposure)
        loss_ref[:, cols] = jnp.concatenate(out, axis=0).astype(bf16)
    loc_count = lax.axis_size("loc")
    chips = loc_count // CORES
    me = lax.axis_index("loc")
    chip, core = me // CORES, lax.rem(me, CORES)
    loss = loss_ref[...]
    for k in range(chips):
        owner = chip_at(chip, k, chips) * CORES + (1 - core)
        send_ref[k] = block_totals(contract_s, loss, owner * share, share)


def own_kernel(share, contract_s, loss_ref, out_ref):
    chips = out_ref.shape[0]
    me = lax.axis_index("loc")
    chip, core = me // CORES, lax.rem(me, CORES)
    loss = loss_ref[...]
    for k in range(chips):
        owner = chip_at(chip, k, chips) * CORES + core
        out_ref[k] = block_totals(contract_s, loss, owner * share, share)


def year_kernel(starts, *refs):
    count = len(starts)
    ins, (terms_ref, year_ref), outs = (
        refs[:count], refs[count : count + 2], refs[count + 2 :]
    )
    events = ins[0].shape[0]
    bounds = sorted(set(starts) | {events})
    rows = []
    for low, high in zip(bounds, bounds[1:]):
        inside = [
            ref[low - start : high - start, :]
            for start, ref in zip(starts, ins)
            if start <= low and start + ref.shape[0] >= high
        ]
        rows.append(functools.reduce(jnp.add, inside))
    total = jnp.concatenate(rows, axis=0)
    occurrence = jnp.minimum(jnp.maximum(total - terms_ref[0:1, :], 0.0), terms_ref[1:2, :])
    evs = len(outs)
    ev = lax.axis_index("ev")
    for m, out in enumerate(outs):
        first = lax.rem(ev + m, evs) * YR_DEV
        years = lax.broadcasted_iota(i32, (YR_DEV, events), 0) + first
        onehot = (years == year_ref[...]).astype(f32)
        out[...] = jnp.dot(
            onehot, occurrence, precision=lax.Precision.HIGHEST, preferred_element_type=f32
        )


def annual_of(ins, terms_ref):
    yearly = functools.reduce(jnp.add, [ref[...] for ref in ins])
    return jnp.minimum(jnp.maximum(yearly - terms_ref[2:3, :], 0.0), terms_ref[3:4, :])


def part_kernel(*refs):
    *ins, terms_ref, part_ref = refs
    annual = annual_of(ins, terms_ref)
    part = lax.dot_general(
        jnp.ones((SUBLANES, annual.shape[1]), f32), annual, (((1,), (1,)), ((), ())),
        precision=lax.Precision.HIGHEST, preferred_element_type=f32,
    )
    part_ref[...] = part[0:1, :]


def annual_kernel(*refs):
    *ins, terms_ref, annual_ref = refs
    annual_ref[...] = annual_of(ins, terms_ref)


def params(mib):
    return pltpu.CompilerParams(vmem_limit_bytes=mib << 20)


def rotate(size, k):
    return [(i, (i + k) % size) for i in range(size)]


def z_pairs(size, offset, only=None):
    chips = size // CORES
    return [
        (
            chip * CORES + core,
            ((chip ^ offset) if chips & (chips - 1) == 0 else (chip + offset) % chips) * CORES
            + core,
        )
        for chip in (range(chips) if only is None else only)
        for core in range(CORES)
    ]


def exchange(own, got):
    size = lax.axis_size("loc")
    chips, events, _ = own.shape

    def part(k, rows):
        return own[k, rows] + got[k, rows]

    every = slice(0, events)
    if not (HYBRID and chips == 4 and events % (2 * SUBLANES) == 0):
        return [
            (0, lax.ppermute(part(k, every), "loc", z_pairs(size, k)))
            for k in range(chips - 1, 0, -1)
        ]
    ahead, rest = slice(0, events // 2), slice(events // 2, events)
    far, mid = part(2, ahead), part(3, ahead)
    relay = lax.ppermute(jnp.concatenate([mid, far]), "loc", z_pairs(size, 1, (0, 3)))
    late3 = lax.ppermute(part(3, rest), "loc", z_pairs(size, 3))
    late2 = lax.ppermute(part(2, rest), "loc", z_pairs(size, 2))
    near = lax.ppermute(part(1, every), "loc", z_pairs(size, 1))
    half = events // 2
    mid = lax.ppermute(mid + relay[half:], "loc", z_pairs(size, 3, (1, 2)))
    far = lax.ppermute(far + relay[:half], "loc", z_pairs(size, 2, (1, 2)))
    return [(0, near), (half, late3), (half, late2), (0, mid), (0, far)]


def mean_over_loc(part):
    size = lax.axis_size("loc")
    if size & (size - 1) or size < 2 * CORES:
        return lax.psum(part, "loc")

    def swap(x, k):
        return lax.ppermute(x, "loc", [(i, i ^ k) for i in range(size)])

    total = (part + swap(part, 1)) + (swap(part, 2) + swap(part, 3))
    step = 4
    while step < size:
        total = total + swap(total, step)
        step *= 2
    return total


def local(
    intensity_bin, bin_fraction, footprint_mask, location_contract, location_class, exposure,
    curves, event_year, occ_retention, occ_limit, agg_retention, agg_limit,
):
    events, locations = intensity_bin.shape
    curve_count, knots = curves.shape
    contract_count = occ_retention.shape[0]
    loc_count = lax.axis_size("loc")
    evs = lax.axis_size("ev")
    chips = loc_count // CORES
    share = contract_count // loc_count
    tiles = locations // LANES
    parts = 4
    dma = pltpu.SemaphoreType.DMA
    send, loss, contract_v, year_v = pl.pallas_call(
        functools.partial(damage_kernel, share, parts),
        out_shape=(
            jax.ShapeDtypeStruct((chips, events, share), f32),
            jax.ShapeDtypeStruct((events, locations), bf16),
            jax.ShapeDtypeStruct((tiles, LANES), i32),
            jax.ShapeDtypeStruct((1, events), i32),
        ),
        in_specs=[HBM] * 8,
        out_specs=(VMEM,) * 4,
        scratch_shapes=[
            pltpu.VMEM((events, locations), i32),
            pltpu.VMEM((events, locations), bf16),
            pltpu.VMEM((tiles, events), i32),
            pltpu.VMEM((tiles, LANES), i32),
            pltpu.VMEM((tiles, LANES), f32),
            pltpu.VMEM((knots, curve_count), f32),
            pltpu.VMEM((2 * knots, locations), f32),
            dma((6 + 2 * parts,)),
        ],
        compiler_params=params(24),
        cost_estimate=pl.CostEstimate(flops=10**9, bytes_accessed=2 << 20, transcendentals=0),
        name="damage",
    )(
        *(
            pltpu.with_memory_space_constraint(x, pltpu.HBM)
            for x in (
                intensity_bin, bin_fraction, footprint_mask.T,
                location_class.reshape(tiles, LANES), exposure.reshape(tiles, LANES), curves.T,
                location_contract.reshape(tiles, LANES), event_year.reshape(1, events),
            )
        )
    )
    partner = [(i, i ^ 1) for i in range(loc_count)]
    got = lax.ppermute(send, "loc", partner)
    own = pl.pallas_call(
        functools.partial(own_kernel, share),
        out_shape=jax.ShapeDtypeStruct((chips, events, share), f32),
        in_specs=[VMEM, VMEM],
        out_specs=VMEM,
        compiler_params=params(16),
        cost_estimate=pl.CostEstimate(flops=10**9, bytes_accessed=2 << 20, transcendentals=0),
        name="own_part",
    )(contract_v, loss)
    starts, blocks = zip(*([(0, own[0]), (0, got[0])] + exchange(own, got)))
    first = lax.axis_index("loc") * share
    terms = lax.dynamic_slice(
        jnp.stack([occ_retention, occ_limit, agg_retention, agg_limit]), (0, first), (4, share)
    )
    yearly = pl.pallas_call(
        functools.partial(year_kernel, starts),
        out_shape=tuple(jax.ShapeDtypeStruct((YR_DEV, share), f32) for _ in range(evs)),
        in_specs=[VMEM] * (len(blocks) + 2),
        out_specs=tuple(VMEM for _ in range(evs)),
        compiler_params=params(16),
        name="years",
    )(*blocks, terms, year_v)
    sums = [yearly[0]] + [
        lax.ppermute(yearly[m], "ev", rotate(evs, m)) for m in range(1, evs)
    ]
    part = pl.pallas_call(
        part_kernel,
        out_shape=jax.ShapeDtypeStruct((1, YR_DEV), f32),
        in_specs=[VMEM] * (len(sums) + 1),
        out_specs=VMEM,
        compiler_params=params(8),
        name="mean_part",
    )(*sums, terms)
    mean = mean_over_loc(part.reshape(YR_DEV))
    annual = pl.pallas_call(
        annual_kernel,
        out_shape=jax.ShapeDtypeStruct((YR_DEV, share), f32),
        in_specs=[VMEM] * (len(sums) + 1),
        out_specs=VMEM,
        compiler_params=params(8),
        cost_estimate=pl.CostEstimate(flops=10**6, bytes_accessed=1 << 20, transcendentals=0),
        name="annual",
    )(*sums, terms)
    return annual.T, mean / contract_count


def solution(mesh):
    in_specs = (
        P("ev", ("grp", "loc")),
        P("ev", ("grp", "loc")),
        P("ev", ("grp", "loc")),
        P(("grp", "loc")),
        P(("grp", "loc")),
        P(("grp", "loc")),
        P(),
        P("ev"),
        P("grp"),
        P("grp"),
        P("grp"),
        P("grp"),
    )
    out_specs = (P(("grp", "loc"), "ev"), P(("grp", "ev")))
    return jax.shard_map(local, mesh=mesh, in_specs=in_specs, out_specs=out_specs, check_vma=False)
```
